32 devices in a mesh: head: 8 (over y, x, core), req: 4 (over z).
Axes of the slice: x: 2, y: 2, z: 4, core: 2. Of those that a mesh axis runs over, the one named last changes fastest.
Arguments:
- hidden: bfloat16 [128, 5, 2048], P('req', None, 'head'), may hold values from -6 to 6
- w_key: bfloat16 [2048, 4096], P('head'), may hold values from -0.125 to 0.125
- w_value: bfloat16 [2048, 32, 256], P(None, 'head'), may hold values from -0.125 to 0.125
- w_gates: bfloat16 [2048, 32, 2], P(None, 'head'), may hold values from -0.125 to 0.125
- conv_key: bfloat16 [4, 4096], replicated, may hold values from -3 to 3
- conv_value: bfloat16 [4, 4096], P(None, 'head'), may hold values from -3 to 3
- key_conv_state: bfloat16 [128, 3, 4096], P('req'), may hold values from -6 to 6
- value_conv_state: bfloat16 [128, 3, 4096], P('req', None, 'head'), may hold values from -6 to 6
- states: float32 [128, 32, 128, 128], P('req', 'head'), may hold values from -3 to 3
- a_log: float32 [32], P('head'), may hold values from -1.5 to 1
- dt_bias: float32 [32], P('head'), may hold values from -1 to 1
- norm_weight: float32 [128], replicated, may hold values from 0.1 to 1.9
- w_out: bfloat16 [4096, 2048], P('head'), may hold values from -0.125 to 0.125
- accepted: int32 [128], P('req'), may hold values from 0 to 4
- next_group: int32 [128], P('req'), may hold values from 0 to 3, as said below
- next_slot: int32 [128], P('req'), may hold values from 0 to 31, as said below
Outputs:
- mixed: bfloat16 [128, 5, 2048], P('req', None, 'head')
- new_states: float32 [128, 32, 128, 128], P('req', 'head')
- new_key_conv: bfloat16 [128, 3, 4096], P('req', None, 'head')
- new_value_conv: bfloat16 [128, 3, 4096], P('req', None, 'head')
The draws below stay inside these ranges and needn't reach their ends.
Inputs may be any that keep to these rules, and one draw needn't show every extreme that they name: `next_group`: within each group's 32 requests at most 12 have the same next group, and in every draw some group sends exactly 12 to one group; every group is named by exactly 32 requests in all. The pairs (next_group, next_slot) are all different.
All inputs are finite; a program needn't handle non-finite values.
Results may differ from the reference program's by a relative error of at most 0.012.
Values may be sent and summed in bfloat16 or wider, within the bound.
A program may use at most 128 MiB of HBM per device.

```python
import jax
import jax.numpy as jnp
from jax import lax

D = 2048
HK = 16
HV = 32
DK = 128
DV = 128
KS = 4
R_DEV = 32
W = 5
CAP = 12
REQUESTS = 128
N_REQ = 4


def owner_plan(key):
    base_key = jax.random.fold_in(key, 7)
    key_delta, key_shift, key_order, key_slots = jax.random.split(base_key, 4)
    leftover = R_DEV - CAP
    share = leftover // (N_REQ - 1)
    excess = leftover - share * (N_REQ - 1)
    counts = jnp.full((N_REQ,), share, jnp.int32).at[0].set(CAP).at[N_REQ - 1].add(excess)
    moved = jax.random.randint(key_delta, (), 0, share // 2 + 1).astype(jnp.int32)
    counts = counts.at[1].add(-moved).at[2].add(moved)
    offset = jax.random.randint(key_shift, (), 0, N_REQ).astype(jnp.int32)
    source = jnp.arange(N_REQ, dtype=jnp.int32)[:, None]
    target = jnp.arange(N_REQ, dtype=jnp.int32)[None, :]
    table = counts[(target - source - offset) % N_REQ]
    bounds = jnp.cumsum(table, axis=1)
    position = jnp.arange(R_DEV, dtype=jnp.int32)
    ordered = jnp.sum((position[None, :, None] >= bounds[:, None, :]).astype(jnp.int32), axis=2)
    orders = jax.vmap(lambda sub: jax.random.permutation(sub, R_DEV))(jax.random.split(key_order, N_REQ))
    destination = jnp.take_along_axis(ordered, orders.astype(jnp.int32), axis=1).reshape(-1)
    onehot = (destination[:, None] == jnp.arange(N_REQ, dtype=jnp.int32)[None, :]).astype(jnp.int32)
    before = jnp.cumsum(onehot, axis=0) - onehot
    rank = jnp.sum(before * onehot, axis=1)
    slot_tables = jax.vmap(lambda sub: jax.random.permutation(sub, R_DEV))(jax.random.split(key_slots, N_REQ)).astype(jnp.int32)
    slots = slot_tables[destination, rank]
    return (destination.astype(jnp.int32), slots.astype(jnp.int32))


def draw_next_group(key, part):
    return owner_plan(key)[0]


def draw_next_slot(key, part):
    return owner_plan(key)[1]


def set_ends(entries, stream_key, smallest, largest):
    longest = entries.shape.index(max(entries.shape))
    spots = []
    for shift in (0, 1):
        where = [jax.random.randint(jax.random.fold_in(stream_key, axis), (), 0, length) for axis, length in enumerate(entries.shape)]
        where[longest] = (where[longest] + shift) % entries.shape[longest]
        spots.append(tuple(where))
    return entries.at[spots[0]].set(smallest).at[spots[1]].set(largest)


def raised(drawn, own_key, source, target, blocks, factor):
    owner, partner = [(jnp.arange(drawn.shape[dim]) // (drawn.shape[dim] // blocks)).reshape([-1 if axis == dim else 1 for axis in range(drawn.ndim)]) for dim in (source, target)]
    chosen = jax.random.permutation(own_key, blocks)[partner]
    strong = (owner == chosen) | (owner == (partner + blocks // 2) % blocks)
    return jnp.where(strong, factor * drawn, drawn)


def shard_levels(key, extent, cuts, low, high):
    gain = 1.0
    for dim, shards_of in cuts:
        steps = jax.random.uniform(jax.random.fold_in(jax.random.fold_in(key, 6), dim), (shards_of,), jnp.float32, low / len(cuts), high / len(cuts))
        gain = gain * jnp.repeat(jnp.exp(steps), extent[dim] // shards_of).reshape((-1,) + (1,) * (len(extent) - 1 - dim))
    return gain


def gaussian(stream_key, shape, width, reach, cuts=(), kind=jnp.bfloat16):
    result = jax.random.normal(stream_key, shape, jnp.float32) * width
    if len(cuts) > 0:
        result = shard_levels(stream_key, shape, cuts, -0.22, 0.18) * result
    return jnp.clip(result, min=-reach, max=reach).astype(kind)


def heavy_noise(rng, dims, width, limit, cuts, heavy, kind=jnp.bfloat16):
    drawn = width * jax.random.normal(rng, dims, jnp.float32)
    if cuts:
        drawn = drawn * shard_levels(rng, dims, cuts, -0.22, 0.18)
    return jnp.clip(raised(drawn, jax.random.fold_in(rng, 3), *heavy), -limit, limit).astype(kind)


def setup_inputs(seed: int = 0) -> dict:
    keys = jax.random.split(jax.random.key(seed), 17)
    return {
        "hidden": gaussian(keys[0], (REQUESTS, W, D), 1.0, 6.0, ((0, 4), (2, 8))),
        "w_key": gaussian(keys[1], (D, HK * 2 * DK), D ** -0.5, 0.125, ((0, 8),)),
        "w_value": gaussian(keys[2], (D, HV, 2 * DV), D ** -0.5, 0.125, ((1, 8),)),
        "w_gates": gaussian(keys[3], (D, HV, 2), D ** -0.5, 0.125, ((1, 8),)),
        "conv_key": gaussian(keys[4], (KS, HK * 2 * DK), KS ** -0.5, 3.0),
        "conv_value": gaussian(keys[5], (KS, HV * DV), KS ** -0.5, 3.0, ((1, 8),)),
        "key_conv_state": gaussian(keys[6], (REQUESTS, KS - 1, HK * 2 * DK), 1.0, 6.0, ((0, 4),)),
        "value_conv_state": gaussian(keys[7], (REQUESTS, KS - 1, HV * DV), 1.0, 6.0, ((0, 4), (2, 8))),
        "states": gaussian(keys[8], (REQUESTS, HV, DK, DV), 0.5, 3.0, ((0, 4), (1, 8)), jnp.float32),
        "a_log": jnp.clip(-1.5 + 2.5 * jax.random.uniform(keys[9], (HV,), jnp.float32) ** shard_levels(keys[9], (HV,), ((0, 8),), -0.2, 0.2), -1.5, 1.0),
        "dt_bias": jnp.clip(jax.random.uniform(keys[10], (HV,), jnp.float32, -1.0, 1.0) * shard_levels(keys[10], (HV,), ((0, 8),), -0.4, 0.0), -1.0, 1.0),
        "norm_weight": jnp.clip(1.0 + 0.18 * jax.random.normal(keys[11], (DV,), jnp.float32), 0.1, 1.9),
        "w_out": heavy_noise(keys[12], (HV * DV, D), (HV * DV) ** -0.5, 0.125, ((0, 8),), (0, 1, 8, 2.0)),
        "accepted": set_ends(jax.random.randint(keys[13], (REQUESTS,), 0, W), jax.random.fold_in(keys[13], 1), 0, W - 1).astype(jnp.int32),
        "next_group": draw_next_group(jax.random.fold_in(keys[16], 71), 0),
        "next_slot": draw_next_slot(jax.random.fold_in(keys[16], 71), 0),
    }


def causal_conv(state, raw, taps):
    joined = jnp.concatenate([state, raw], axis=1)
    wide = joined.astype(jnp.float32)
    kernel = taps.astype(jnp.float32)
    total = kernel[0][None, None, :] * wide[:, 0:W]
    for index in range(1, KS):
        total = total + kernel[index][None, None, :] * wide[:, index:index + W]
    return (jax.nn.silu(total).astype(jnp.bfloat16), joined)

def keep_tail(joined, accepted):
    offsets = accepted[:, None] + 1 + jnp.arange(KS - 1, dtype=jnp.int32)[None, :]
    return jnp.take_along_axis(joined, offsets[:, :, None], axis=1)

def unit_norm(vector):
    return vector * lax.rsqrt(lax.optimization_barrier(jnp.sum(vector * vector, axis=-1, keepdims=True)) + 1e-06)

def reference(hidden, w_key, w_value, w_gates, conv_key, conv_value, key_conv_state, value_conv_state, states, a_log, dt_bias, norm_weight, w_out, accepted, next_group, next_slot):
    total_rows = REQUESTS * W
    flat = hidden.reshape(total_rows, D)
    keys_raw = jnp.dot(flat, w_key, preferred_element_type=jnp.float32).astype(jnp.bfloat16)
    keys_raw = keys_raw.reshape(REQUESTS, W, HK * 2 * DK)
    value_raw = jnp.dot(flat, w_value.reshape(D, HV * 2 * DV), preferred_element_type=jnp.float32).astype(jnp.bfloat16)
    value_raw = value_raw.reshape(REQUESTS, W, HV, 2, DV)
    gate_raw = jnp.dot(flat, w_gates.reshape(D, HV * 2), preferred_element_type=jnp.float32).astype(jnp.bfloat16)
    gate_raw = gate_raw.reshape(REQUESTS, W, HV, 2).astype(jnp.float32)
    key_out, key_joined = causal_conv(key_conv_state, keys_raw, conv_key)
    v_raw = value_raw[:, :, :, 0].reshape(REQUESTS, W, HV * DV)
    value_out, value_joined = causal_conv(value_conv_state, v_raw, conv_value)
    split = key_out.reshape(REQUESTS, W, HK, 2, DK).astype(jnp.float32)
    queries = unit_norm(split[:, :, :, 0]) * DK ** (-0.5)
    key_rows = unit_norm(split[:, :, :, 1])
    queries = jnp.repeat(queries, HV // HK, axis=2)
    key_rows = jnp.repeat(key_rows, HV // HK, axis=2)
    values = value_out.reshape(REQUESTS, W, HV, DV).astype(jnp.float32)
    beta = jax.nn.sigmoid(gate_raw[..., 0])
    decay = jnp.exp(-jnp.exp(a_log) * jax.nn.softplus(gate_raw[..., 1] + dt_bias))

    def one_head(pieces):
        q_head, k_head, v_head, b_head, d_head, s_head = pieces
        current = s_head
        chosen = s_head
        outputs = []
        for step in range(W):
            current = current * d_head[:, step][:, None, None]
            guess = jnp.einsum('rk,rkv->rv', k_head[:, step], current, precision=lax.Precision.HIGHEST)
            change = b_head[:, step][:, None] * (v_head[:, step] - guess)
            current = current + k_head[:, step][:, :, None] * change[:, None, :]
            outputs.append(jnp.einsum('rk,rkv->rv', q_head[:, step], current, precision=lax.Precision.HIGHEST))
            chosen = jnp.where((accepted == step)[:, None, None], current, chosen)
        return (jnp.stack(outputs, axis=1), chosen)
    core, kept = lax.map(one_head, (jnp.moveaxis(queries, 2, 0), jnp.moveaxis(key_rows, 2, 0), jnp.moveaxis(values, 2, 0), jnp.moveaxis(beta, 2, 0), jnp.moveaxis(decay, 2, 0), jnp.moveaxis(states, 1, 0)))
    core = jnp.moveaxis(core, 0, 2)
    kept = jnp.moveaxis(kept, 0, 1)
    zgate = value_raw[:, :, :, 1].astype(jnp.float32)
    scaled = core * lax.rsqrt(lax.optimization_barrier(jnp.mean(core * core, axis=-1, keepdims=True)) + 1e-06)
    normed = (scaled * norm_weight * jax.nn.silu(zgate)).astype(jnp.bfloat16)
    mixed = jnp.dot(normed.reshape(total_rows, HV * DV), w_out, preferred_element_type=jnp.float32).astype(jnp.bfloat16)
    mixed = mixed.reshape(REQUESTS, W, D)
    key_tail = keep_tail(key_joined, accepted)
    value_tail = keep_tail(value_joined, accepted)
    target = (next_group * R_DEV + next_slot).astype(jnp.int32)
    new_states = jnp.zeros_like(states).at[target].set(kept)
    new_key_conv = jnp.zeros_like(key_conv_state).at[target].set(key_tail)
    new_value_conv = jnp.zeros_like(value_conv_state).at[target].set(value_tail)
    return (mixed, new_states, new_key_conv, new_value_conv)
```

```python
import functools

import jax
import jax.numpy as jnp
from jax import lax
from jax.experimental import pallas as pl
from jax.experimental.pallas import tpu as pltpu
from jax.sharding import PartitionSpec as P

CAP = 12
F32 = jnp.float32
BF16 = jnp.bfloat16


def spread_heads(block, devices, key_heads, pair_width):
    rows = block.shape[0]
    shaped = block.reshape(rows, -1, pair_width)
    wanted = devices * key_heads
    if shaped.shape[1] < wanted:
        shaped = jnp.repeat(shaped, wanted // shaped.shape[1], axis=1)
    return shaped.reshape(rows, wanted * pair_width)


def silu(x):
    return x / (1.0 + jnp.exp(-x))


def pack_kernel(index_ref, in_ref, out_ref):
    out_ref[...] = in_ref[...].astype(out_ref.dtype)


def pack(states, picked):
    count = picked.shape[0]
    block = (1,) + states.shape[1:]
    zeros = (0,) * (states.ndim - 1)
    return pl.pallas_call(
        pack_kernel,
        out_shape=jax.ShapeDtypeStruct((count,) + states.shape[1:], BF16),
        grid_spec=pltpu.PrefetchScalarGridSpec(
            num_scalar_prefetch=1,
            grid=(count,),
            in_specs=[pl.BlockSpec(block, lambda i, index: (index[i],) + zeros)],
            out_specs=pl.BlockSpec(block, lambda i, index: (i,) + zeros),
        ),
        name="pack_states",
    )(picked, states)


def layout(key_heads, heads, window, span, size, needed):
    keys = 0
    deltas = keys + key_heads * window * size
    scale = deltas + heads * window * size
    key_tail = scale + heads * size
    value_tail = key_tail + span * needed
    return keys, deltas, scale, key_tail, value_tail, value_tail + span * heads * size


def verify_kernel(
    dims,
    x_ref,
    wk_ref,
    wv_ref,
    wg_ref,
    ck_ref,
    cv_ref,
    ks_ref,
    vs_ref,
    al_ref,
    db_ref,
    nw_ref,
    acc_ref,
    oh_ref,
    st_ref,
    normed_ref,
    pay_ref,
    kq_s,
    g_s,
    v_s,
    z_s,
    beta_s,
    decay_s,
    p_s,
):
    requests, window, heads, key_heads, size, span, needed, batch, slots = dims
    half = slots // 2
    ratio = heads // key_heads
    devices, _, piece = x_ref.shape
    o_key, o_delta, o_scale, o_kt, o_vt, _ = layout(key_heads, heads, window, span, size, needed)
    step = pl.program_id(0)

    def project(w_ref, lo, width):
        total = jnp.dot(
            x_ref[0], w_ref[0:piece, lo : lo + width], preferred_element_type=F32
        )
        for d in range(1, devices):
            total = total + jnp.dot(
                x_ref[d],
                w_ref[d * piece : (d + 1) * piece, lo : lo + width],
                preferred_element_type=F32,
            )
        return total.astype(BF16).astype(F32)

    def conv(state_ref, taps_ref, raw, lo, width, tail_at, tail_width):
        u = [state_ref[i, :, lo : lo + width].astype(F32) for i in range(span)]
        u += [raw[t * requests : (t + 1) * requests] for t in range(window)]
        outs = []
        for t in range(window):
            total = taps_ref[0:1, lo : lo + width].astype(F32) * u[t]
            for i in range(1, span + 1):
                total = total + taps_ref[i : i + 1, lo : lo + width].astype(F32) * u[t + i]
            outs.append(silu(total).astype(BF16).astype(F32))
        accepted = acc_ref[...]
        for i in range(span):
            tail = u[1 + i]
            for a in range(1, window):
                tail = jnp.where(accepted == a, u[a + 1 + i], tail)
            at = tail_at + i * tail_width + lo
            p_s[:, at : at + width] = tail.astype(BF16)
        return outs

    @pl.when(step == 0)
    def _():
        kq_s[...] = jnp.zeros_like(kq_s)
        for kh in range(key_heads):
            width = 2 * size
            raw = project(wk_ref, kh * width, width)
            outs = conv(ks_ref, ck_ref, raw, kh * width, width, o_kt, needed)
            for t in range(window):
                q = outs[t][:, :size]
                k = outs[t][:, size:]
                q = q * lax.rsqrt(jnp.sum(q * q, axis=-1, keepdims=True) + 1e-06)
                k = k * lax.rsqrt(jnp.sum(k * k, axis=-1, keepdims=True) + 1e-06)
                kq_s[kh, pl.ds(t, requests, stride=slots), :] = k
                kq_s[kh, pl.ds(half + t, requests, stride=slots), :] = q * size ** (-0.5)
        for h in range(heads):
            raw = project(wv_ref, h * 2 * size, 2 * size)
            zg = raw[:, size:]
            z_s[:, h * size : (h + 1) * size] = silu(zg)
            outs = conv(vs_ref, cv_ref, raw[:, :size], h * size, size, o_vt, heads * size)
            for t in range(window):
                v_s[t * requests : (t + 1) * requests, h * size : (h + 1) * size] = outs[t]
        gates = project(wg_ref, 0, 2 * heads)
        beta_s[...] = 1.0 / (1.0 + jnp.exp(-gates))
        shifted = gates + db_ref[...]
        soft = jnp.maximum(shifted, 0.0) + jnp.log1p(jnp.exp(-jnp.abs(shifted)))
        decay_s[...] = jnp.exp(-jnp.exp(al_ref[...]) * soft)

    for rr in range(batch):
        row = pl.multiple_of((step * batch + rr) * slots, slots)
        for kh in range(key_heads):
            lhs = kq_s[kh, pl.ds(row, slots), :].astype(BF16)
            rhs = jnp.concatenate(
                [st_ref[rr, kh * ratio + e].astype(BF16) for e in range(ratio)], axis=1
            )
            got = jnp.dot(lhs, rhs, preferred_element_type=F32)
            for e in range(ratio):
                g_s[kh * ratio + e, pl.ds(row, slots), :] = got[:, e * size : (e + 1) * size]

    @pl.when(step == pl.num_programs(0) - 1)
    def _():
        accepted = acc_ref[...]
        gain = nw_ref[...]
        for kh in range(key_heads):
            ks = [kq_s[kh, pl.ds(t, requests, stride=slots), :] for t in range(window)]
            qs = [kq_s[kh, pl.ds(half + t, requests, stride=slots), :] for t in range(window)]
            kk = {}
            kq = {}
            for t in range(window):
                at = o_key + (kh * window + t) * size
                p_s[:, at : at + size] = ks[t].astype(BF16)
                for j in range(t + 1):
                    if j < t:
                        kk[t, j] = jnp.sum(ks[t] * ks[j], axis=-1, keepdims=True)
                    kq[t, j] = jnp.sum(qs[t] * ks[j], axis=-1, keepdims=True)
            for e in range(ratio):
                h = kh * ratio + e
                cols = slice(h * size, (h + 1) * size)
                deltas = []
                coef = []
                whole = None
                kept_coef = [None] * window
                kept_whole = None
                for t in range(window):
                    rows = slice(t * requests, (t + 1) * requests)
                    beta = beta_s[rows, 2 * h : 2 * h + 1]
                    decay = decay_s[rows, 2 * h + 1 : 2 * h + 2]
                    whole = decay if t == 0 else whole * decay
                    coef = [c * decay for c in coef]
                    guess = whole * g_s[h, pl.ds(t, requests, stride=slots), :]
                    core = whole * g_s[h, pl.ds(half + t, requests, stride=slots), :]
                    for j in range(t):
                        guess = guess + (coef[j] * kk[t, j]) * deltas[j]
                        core = core + (coef[j] * kq[t, j]) * deltas[j]
                    delta = beta * (v_s[rows, cols] - guess)
                    core = core + kq[t, t] * delta
                    deltas.append(delta)
                    coef.append(jnp.ones_like(decay))
                    here = accepted == t
                    kept_whole = whole if t == 0 else jnp.where(here, whole, kept_whole)
                    for j in range(t + 1):
                        before = kept_coef[j] if kept_coef[j] is not None else jnp.zeros_like(decay)
                        kept_coef[j] = jnp.where(here, coef[j], before)
                    scaled = core * lax.rsqrt(
                        jnp.mean(core * core, axis=-1, keepdims=True) + 1e-06
                    )
                    normed_ref[rows, cols] = (scaled * gain * z_s[rows, cols]).astype(BF16)
                for j in range(window):
                    at = o_delta + (h * window + j) * size
                    p_s[:, at : at + size] = (kept_coef[j] * deltas[j]).astype(BF16)
                at = o_scale + h * size
                p_s[:, at : at + size] = jnp.broadcast_to(kept_whole, (requests, size)).astype(BF16)
        pay_ref[...] = jnp.dot(oh_ref[...], p_s[...], preferred_element_type=F32).astype(BF16)


def verify(dims, x, wk, wv, wg, ck, cv, ks, vs, al, db, nw, acc, oh, states):
    requests, window, heads, key_heads, size, span, needed, batch, slots = dims
    rows = requests * window
    width = layout(key_heads, heads, window, span, size, needed)[-1]
    small = [x, wk, wv, wg, ck, cv, ks, vs, al, db, nw, acc, oh]

    def whole(shape):
        return pl.BlockSpec(
            shape, lambda i, n=len(shape): (0,) * n, pipeline_mode=pl.Buffered(1)
        )

    return pl.pallas_call(
        functools.partial(verify_kernel, dims),
        out_shape=(
            jax.ShapeDtypeStruct((rows, heads * size), BF16),
            jax.ShapeDtypeStruct((oh.shape[0], width), BF16),
        ),
        grid=(requests // batch,),
        in_specs=[whole(a.shape) for a in small]
        + [pl.BlockSpec((batch,) + states.shape[1:], lambda i: (i, 0, 0, 0))],
        out_specs=(
            pl.BlockSpec((rows, heads * size), lambda i: (0, 0)),
            pl.BlockSpec((oh.shape[0], width), lambda i: (0, 0)),
        ),
        scratch_shapes=[
            pltpu.VMEM((key_heads, requests * slots, size), F32),
            pltpu.VMEM((heads, requests * slots, size), F32),
            pltpu.VMEM((rows, heads * size), F32),
            pltpu.VMEM((rows, heads * size), F32),
            pltpu.VMEM((rows, 2 * heads), F32),
            pltpu.VMEM((rows, 2 * heads), F32),
            pltpu.VMEM((requests, width), BF16),
        ],
        compiler_params=pltpu.CompilerParams(vmem_limit_bytes=40 * 1024 * 1024),
        name="verify_window",
    )(*small, states)


def place_kernel(
    dims,
    kind_ref,
    own_index,
    base_index,
    extra_index,
    oh_ref,
    pay_ref,
    st_ref,
    base_ref,
    extra_ref,
    out_ref,
    kt_ref,
    vt_ref,
    k_s,
    d_s,
    w_s,
):
    requests, window, heads, key_heads, size, span, needed, lines = dims
    ratio = heads // key_heads
    o_key, o_delta, o_scale, o_kt, o_vt, width = layout(
        key_heads, heads, window, span, size, needed
    )
    step = pl.program_id(0)

    @pl.when(step == 0)
    def _():
        k_s[...] = jnp.zeros_like(k_s)
        d_s[...] = jnp.zeros_like(d_s)

        def columns(lo, hi):
            return jnp.dot(oh_ref[...], pay_ref[:, lo:hi], preferred_element_type=F32)

        for kh in range(key_heads):
            for j in range(window):
                at = o_key + (kh * window + j) * size
                k_s[kh, pl.ds(j, requests, stride=lines), :] = columns(at, at + size)
        for h in range(heads):
            for j in range(window):
                at = o_delta + (h * window + j) * size
                d_s[h, pl.ds(j, requests, stride=lines), :] = columns(at, at + size)
            at = o_scale + h * size
            w_s[h] = columns(at, at + size)
        kt_ref[...] = columns(o_kt, o_vt).astype(BF16)
        vt_ref[...] = columns(o_vt, width).astype(BF16)

    def apply(source_ref):
        row = pl.multiple_of(step * lines, lines)
        for h in range(heads):
            k = k_s[h // ratio, pl.ds(row, lines), :].astype(BF16)
            d = d_s[h, pl.ds(row, lines), :].astype(BF16)
            update = lax.dot_general(
                k, d, (((0,), (0,)), ((), ())), preferred_element_type=F32
            )
            weight = w_s[h, pl.ds(step, 1), :]
            out_ref[0, h] = weight * source_ref[0, h].astype(F32) + update

    kind = kind_ref[step]
    for value, source_ref in enumerate((st_ref, base_ref, extra_ref)):

        @pl.when(kind == value)
        def _(source_ref=source_ref):
            apply(source_ref)


def place(dims, kind, own_i, base_i, extra_i, oh, pay, states, base, extra):
    requests, window, heads, key_heads, size, span, needed, lines = dims
    block = (1,) + states.shape[1:]

    def whole(shape):
        return pl.BlockSpec(
            shape, lambda i, *_, n=len(shape): (0,) * n, pipeline_mode=pl.Buffered(1)
        )

    return pl.pallas_call(
        functools.partial(place_kernel, dims),
        out_shape=(
            jax.ShapeDtypeStruct(states.shape, F32),
            jax.ShapeDtypeStruct((requests, span * needed), BF16),
            jax.ShapeDtypeStruct((requests, span * heads * size), BF16),
        ),
        grid_spec=pltpu.PrefetchScalarGridSpec(
            num_scalar_prefetch=4,
            grid=(requests,),
            in_specs=[
                whole(oh.shape),
                whole(pay.shape),
                pl.BlockSpec(block, lambda i, kind, a, b, c: (a[i], 0, 0, 0)),
                pl.BlockSpec(block, lambda i, kind, a, b, c: (b[i], 0, 0, 0)),
                pl.BlockSpec(block, lambda i, kind, a, b, c: (c[i], 0, 0, 0)),
            ],
            out_specs=(
                pl.BlockSpec(block, lambda i, *_: (i, 0, 0, 0)),
                pl.BlockSpec((requests, span * needed), lambda i, *_: (0, 0)),
                pl.BlockSpec((requests, span * heads * size), lambda i, *_: (0, 0)),
            ),
            scratch_shapes=[
                pltpu.VMEM((key_heads, requests * lines, size), F32),
                pltpu.VMEM((heads, requests * lines, size), F32),
                pltpu.VMEM((heads, requests, size), F32),
            ],
        ),
        compiler_params=pltpu.CompilerParams(vmem_limit_bytes=32 * 1024 * 1024),
        name="place_states",
    )(kind, own_i, base_i, extra_i, oh, pay, states, base, extra)


def local(
    hidden,
    w_key,
    w_value,
    w_gates,
    conv_key,
    conv_value,
    key_conv_state,
    value_conv_state,
    states,
    a_log,
    dt_bias,
    norm_weight,
    w_out,
    accepted,
    next_group,
    next_slot,
):
    requests, window, feature_piece = hidden.shape
    rows = requests * window
    heads = states.shape[1]
    size = states.shape[2]
    span = key_conv_state.shape[1]
    devices = lax.axis_size("head")
    position = lax.axis_index("head")
    groups = lax.axis_size("req")
    group = lax.axis_index("req")
    pair_width = 2 * size
    key_heads = max(1, heads // 2)
    needed = key_heads * pair_width
    own_width = key_conv_state.shape[2] // devices
    column_start = (position * heads // 2) * pair_width
    share = min(CAP, requests // groups)
    extra = CAP - share

    onehot = (next_group[:, None] == jnp.arange(groups, dtype=jnp.int32)[None, :]).astype(jnp.int32)
    before = jnp.cumsum(onehot, axis=0) - onehot
    rank = jnp.sum(before * onehot, axis=1)
    matched = (next_group[None, None, :] == jnp.arange(groups, dtype=jnp.int32)[:, None, None]) & (
        rank[None, None, :] == jnp.arange(CAP, dtype=jnp.int32)[None, :, None]
    )
    picked = jnp.sum(
        matched.astype(jnp.int32) * jnp.arange(requests, dtype=jnp.int32)[None, None, :], axis=2
    )

    base_send = pack(states, picked[:, :share].reshape(-1))
    base = lax.all_to_all(base_send, "req", split_axis=0, concat_axis=0, tiled=True)

    gathered = lax.all_gather(jnp.swapaxes(hidden, 0, 1).reshape(rows, feature_piece), "head", axis=0)
    spread = spread_heads(w_key, devices, key_heads, pair_width)
    columns = lax.all_to_all(spread, "head", split_axis=1, concat_axis=0, tiled=True)
    plan = lax.all_gather(jnp.stack([next_group, next_slot]), "req", axis=0)

    local_state = lax.dynamic_slice_in_dim(key_conv_state, column_start, needed, 2)
    local_taps = lax.dynamic_slice_in_dim(conv_key, column_start, needed, 1)
    send_rows = matched.reshape(groups * CAP, requests).astype(BF16)
    dims = (requests, window, heads, key_heads, size, span, needed, min(8, requests), 16)
    normed, pay = verify(
        dims,
        gathered,
        columns,
        w_value.reshape(devices * feature_piece, heads * 2 * size),
        w_gates.reshape(devices * feature_piece, heads * 2),
        local_taps,
        conv_value,
        jnp.swapaxes(local_state, 0, 1),
        jnp.swapaxes(value_conv_state, 0, 1),
        jnp.repeat(a_log, 2)[None, :],
        jnp.repeat(dt_bias, 2)[None, :],
        norm_weight[None, :],
        accepted[:, None],
        send_rows,
        states,
    )
    partial_out = jnp.dot(normed, w_out, preferred_element_type=F32)
    mixed = lax.psum_scatter(partial_out, "head", scatter_dimension=1, tiled=True).astype(BF16)
    mixed = jnp.swapaxes(mixed.reshape(window, requests, -1), 0, 1)
    pay_in = lax.all_to_all(pay, "req", split_axis=0, concat_axis=0, tiled=True)

    groups_of, slots_of = plan[:, 0], plan[:, 1]
    mine = (groups_of == group).astype(jnp.int32)
    ranks = jnp.cumsum(mine, axis=1) - mine
    hit = (mine[None] > 0) & (slots_of[None] == jnp.arange(requests, dtype=jnp.int32)[:, None, None])
    hit = hit.astype(jnp.int32)
    source = jnp.sum(hit * jnp.arange(groups, dtype=jnp.int32)[None, :, None], axis=(1, 2))
    place_rank = jnp.sum(hit * ranks[None], axis=(1, 2))
    origin = jnp.sum(hit * jnp.arange(requests, dtype=jnp.int32)[None, None, :], axis=(1, 2))
    row_of = source * CAP + place_rank
    take_rows = (row_of[:, None] == jnp.arange(groups * CAP, dtype=jnp.int32)[None, :]).astype(BF16)
    kind = jnp.where(source == group, 0, jnp.where(place_rank < share, 1, 2)).astype(jnp.int32)
    shift_in = (group - source + groups) % groups

    counts = jnp.sum(
        (groups_of[:, None, :] == jnp.arange(groups, dtype=jnp.int32)[None, :, None]).astype(
            jnp.int32
        ),
        axis=2,
    )
    shifts = (
        jnp.arange(groups, dtype=jnp.int32)[None, :]
        - jnp.arange(groups, dtype=jnp.int32)[:, None]
        + groups
    ) % groups
    extra_block = (max(extra, 1),) + states.shape[1:]
    late = []
    pick_extra = picked[:, share:]
    pick_extra, counts, partial_out, pay = lax.optimization_barrier(
        (pick_extra, counts, partial_out, pay)
    )
    for shift in range(1, groups):
        most = jnp.max(jnp.where(shifts == shift, counts, 0))
        pairs = [(s, (s + shift) % groups) for s in range(groups)]

        def send(pick, source_states, pairs=pairs, shift=shift):
            rows_out = lax.dynamic_index_in_dim(pick, (group + shift) % groups, 0, keepdims=False)
            return lax.ppermute(pack(source_states, rows_out), "req", pairs)

        def skip(pick, source_states):
            return jnp.zeros(extra_block, BF16)

        if extra > 0:
            late.append(lax.cond(most > share, send, skip, pick_extra, states))
        else:
            late.append(jnp.zeros(extra_block, BF16))
    late = jnp.concatenate(late, axis=0)

    own_i = jnp.where(kind == 0, origin, 0).astype(jnp.int32)
    base_i = jnp.where(kind == 1, source * share + place_rank, 0).astype(jnp.int32)
    extra_i = jnp.where(
        kind == 2, (shift_in - 1) * extra_block[0] + place_rank - share, 0
    ).astype(jnp.int32)
    dims = (requests, window, heads, key_heads, size, span, needed, 8)
    new_states, key_rows, value_rows = place(
        dims, kind, own_i, base_i, extra_i, take_rows, pay_in, states, base, late
    )
    new_key = key_rows.reshape(requests, span, needed)
    if own_width != needed:
        new_key = lax.dynamic_slice_in_dim(
            new_key, position * own_width - column_start, own_width, 2
        )
    new_value = value_rows.reshape(requests, span, heads * size)
    return (mixed, new_states, new_key, new_value)


def solution(mesh):
    in_specs = (
        P("req", None, "head"),
        P("head", None),
        P(None, "head", None),
        P(None, "head", None),
        P(),
        P(None, "head"),
        P("req", None, None),
        P("req", None, "head"),
        P("req", "head", None, None),
        P("head"),
        P("head"),
        P(),
        P("head", None),
        P("req"),
        P("req"),
        P("req"),
    )
    out_specs = (
        P("req", None, "head"),
        P("req", "head", None, None),
        P("req", None, "head"),
        P("req", None, "head"),
    )
    return jax.shard_map(local, mesh=mesh, in_specs=in_specs, out_specs=out_specs, check_vma=False)
```

```python
import functools

import jax
import jax.numpy as jnp
from jax import lax
from jax.experimental import pallas as pl
from jax.experimental.pallas import tpu as pltpu
from jax.sharding import PartitionSpec as P


CAP = 12
F32 = jnp.float32
BF16 = jnp.bfloat16


def spread_heads(block, devices, key_heads, pair_width):
    rows = block.shape[0]
    shaped = block.reshape(rows, -1, pair_width)
    wanted = devices * key_heads
    if shaped.shape[1] < wanted:
        shaped = jnp.repeat(shaped, wanted // shaped.shape[1], axis=1)
    return shaped.reshape(rows, wanted * pair_width)


def silu(x):
    return x / (1.0 + jnp.exp(-x))


def pack_kernel(index_ref, *refs):
    out_ref = refs[-1]
    for row, in_ref in enumerate(refs[:-1]):
        out_ref[row] = in_ref[0].astype(out_ref.dtype)


def pack(states, picked):
    count = picked.shape[0]
    batch = 4 if count % 4 == 0 else 1
    block = states.shape[1:]
    zeros = (0,) * len(block)
    return pl.pallas_call(
        pack_kernel,
        out_shape=jax.ShapeDtypeStruct((count,) + block, BF16),
        grid_spec=pltpu.PrefetchScalarGridSpec(
            num_scalar_prefetch=1,
            grid=(count // batch,),
            in_specs=[
                pl.BlockSpec((1,) + block, lambda i, index, j=j: (index[i * batch + j],) + zeros)
                for j in range(batch)
            ],
            out_specs=pl.BlockSpec((batch,) + block, lambda i, index: (i,) + zeros),
        ),
        name="pack_states",
    )(picked, *([states] * batch))


def layout(key_heads, heads, window, span, size, needed):
    keys = 0
    deltas = keys + key_heads * window * size
    scale = deltas + heads * window * size
    key_tail = scale + heads * size
    value_tail = key_tail + span * needed
    return keys, deltas, scale, key_tail, value_tail, value_tail + span * heads * size


def verify_kernel(
    dims,
    x_ref,
    wk_ref,
    wv_ref,
    wg_ref,
    ck_ref,
    cv_ref,
    ks_ref,
    vs_ref,
    al_ref,
    db_ref,
    nw_ref,
    acc_ref,
    oh_ref,
    plan_ref,
    st_ref,
    normed_ref,
    pay_ref,
    kq_s,
    g_s,
    v_s,
    z_s,
    beta_s,
    decay_s,
    p_s,
):
    requests, window, heads, key_heads, size, span, needed, batch, slots = dims
    half = slots // 2
    ratio = heads // key_heads
    devices, _, piece = x_ref.shape
    o_key, o_delta, o_scale, o_kt, o_vt, _ = layout(key_heads, heads, window, span, size, needed)
    step = pl.program_id(0)

    def project(w_ref, lo, width):
        total = jnp.dot(
            x_ref[0], w_ref[0:piece, lo : lo + width], preferred_element_type=F32
        )
        for d in range(1, devices):
            total = total + jnp.dot(
                x_ref[d],
                w_ref[d * piece : (d + 1) * piece, lo : lo + width],
                preferred_element_type=F32,
            )
        return total.astype(BF16).astype(F32)

    def conv(state_ref, taps_ref, raw, lo, width, tail_at, tail_width):
        u = [state_ref[i, :, lo : lo + width].astype(F32) for i in range(span)]
        u += [raw[t * requests : (t + 1) * requests] for t in range(window)]
        outs = []
        for t in range(window):
            total = taps_ref[0:1, lo : lo + width].astype(F32) * u[t]
            for i in range(1, span + 1):
                total = total + taps_ref[i : i + 1, lo : lo + width].astype(F32) * u[t + i]
            outs.append(silu(total).astype(BF16).astype(F32))
        accepted = acc_ref[...]
        for i in range(span):
            tail = u[1 + i]
            for a in range(1, window):
                tail = jnp.where(accepted == a, u[a + 1 + i], tail)
            at = tail_at + i * tail_width + lo
            p_s[:, at : at + width] = tail.astype(BF16)
        return outs

    @pl.when(step == 0)
    def _():
        kq_s[...] = jnp.zeros_like(kq_s)
        for kh in range(key_heads):
            width = 2 * size
            raw = project(wk_ref, kh * width, width)
            outs = conv(ks_ref, ck_ref, raw, kh * width, width, o_kt, needed)
            for t in range(window):
                q = outs[t][:, :size]
                k = outs[t][:, size:]
                q = q * lax.rsqrt(jnp.sum(q * q, axis=-1, keepdims=True) + 1e-06)
                k = k * lax.rsqrt(jnp.sum(k * k, axis=-1, keepdims=True) + 1e-06)
                kq_s[kh, pl.ds(t, requests, stride=slots), :] = k
                kq_s[kh, pl.ds(half + t, requests, stride=slots), :] = q * size ** (-0.5)
        for h in range(heads):
            raw = project(wv_ref, h * 2 * size, 2 * size)
            zg = raw[:, size:]
            z_s[:, h * size : (h + 1) * size] = silu(zg)
            outs = conv(vs_ref, cv_ref, raw[:, :size], h * size, size, o_vt, heads * size)
            for t in range(window):
                v_s[t * requests : (t + 1) * requests, h * size : (h + 1) * size] = outs[t]
        gates = project(wg_ref, 0, 2 * heads)
        beta_s[...] = 1.0 / (1.0 + jnp.exp(-gates))
        shifted = gates + db_ref[...]
        soft = jnp.maximum(shifted, 0.0) + jnp.log1p(jnp.exp(-jnp.abs(shifted)))
        decay_s[...] = jnp.exp(-jnp.exp(al_ref[...]) * soft)

    for rr in range(batch):
        row = pl.multiple_of((step * batch + rr) * slots, slots)
        for kh in range(key_heads):
            lhs = kq_s[kh, pl.ds(row, slots), :].astype(BF16)
            rhs = jnp.concatenate(
                [st_ref[rr, kh * ratio + e].astype(BF16) for e in range(ratio)], axis=1
            )
            got = jnp.dot(lhs, rhs, preferred_element_type=F32)
            for e in range(ratio):
                g_s[kh * ratio + e, pl.ds(row, slots), :] = got[:, e * size : (e + 1) * size]

    @pl.when(step == pl.num_programs(0) - 1)
    def _():
        accepted = acc_ref[...]
        gain = nw_ref[...]
        for kh in range(key_heads):
            ks = [kq_s[kh, pl.ds(t, requests, stride=slots), :] for t in range(window)]
            qs = [kq_s[kh, pl.ds(half + t, requests, stride=slots), :] for t in range(window)]
            kk = {}
            kq = {}
            for t in range(window):
                at = o_key + (kh * window + t) * size
                p_s[:, at : at + size] = ks[t].astype(BF16)
                for j in range(t + 1):
                    if j < t:
                        kk[t, j] = jnp.sum(ks[t] * ks[j], axis=-1, keepdims=True)
                    kq[t, j] = jnp.sum(qs[t] * ks[j], axis=-1, keepdims=True)
            for e in range(ratio):
                h = kh * ratio + e
                cols = slice(h * size, (h + 1) * size)
                deltas = []
                coef = []
                whole = None
                kept_coef = [None] * window
                kept_whole = None
                for t in range(window):
                    rows = slice(t * requests, (t + 1) * requests)
                    beta = beta_s[rows, 2 * h : 2 * h + 1]
                    decay = decay_s[rows, 2 * h + 1 : 2 * h + 2]
                    whole = decay if t == 0 else whole * decay
                    coef = [c * decay for c in coef]
                    guess = whole * g_s[h, pl.ds(t, requests, stride=slots), :]
                    core = whole * g_s[h, pl.ds(half + t, requests, stride=slots), :]
                    for j in range(t):
                        guess = guess + (coef[j] * kk[t, j]) * deltas[j]
                        core = core + (coef[j] * kq[t, j]) * deltas[j]
                    delta = beta * (v_s[rows, cols] - guess)
                    core = core + kq[t, t] * delta
                    deltas.append(delta)
                    coef.append(jnp.ones_like(decay))
                    here = accepted == t
                    kept_whole = whole if t == 0 else jnp.where(here, whole, kept_whole)
                    for j in range(t + 1):
                        before = kept_coef[j] if kept_coef[j] is not None else jnp.zeros_like(decay)
                        kept_coef[j] = jnp.where(here, coef[j], before)
                    scaled = core * lax.rsqrt(
                        jnp.mean(core * core, axis=-1, keepdims=True) + 1e-06
                    )
                    normed_ref[rows, cols] = (scaled * gain * z_s[rows, cols]).astype(BF16)
                for j in range(window):
                    at = o_delta + (h * window + j) * size
                    p_s[:, at : at + size] = (kept_coef[j] * deltas[j]).astype(BF16)
                at = o_scale + h * size
                p_s[:, at : at + size] = jnp.broadcast_to(kept_whole, (requests, size)).astype(BF16)
        width = p_s.shape[1]
        pay_ref[:, :width] = jnp.dot(oh_ref[...], p_s[...], preferred_element_type=F32).astype(BF16)
        pay_ref[:, width:] = jnp.broadcast_to(
            plan_ref[...], (pay_ref.shape[0], plan_ref.shape[1])
        ).astype(BF16)


def verify(dims, x, wk, wv, wg, ck, cv, ks, vs, al, db, nw, acc, oh, plan, states):
    requests, window, heads, key_heads, size, span, needed, batch, slots = dims
    rows = requests * window
    width = layout(key_heads, heads, window, span, size, needed)[-1]
    small = [x, wk, wv, wg, ck, cv, ks, vs, al, db, nw, acc, oh, plan]
    sent = width + plan.shape[1]

    def whole(shape):
        return pl.BlockSpec(
            shape, lambda i, n=len(shape): (0,) * n, pipeline_mode=pl.Buffered(1)
        )

    return pl.pallas_call(
        functools.partial(verify_kernel, dims),
        out_shape=(
            jax.ShapeDtypeStruct((rows, heads * size), BF16),
            jax.ShapeDtypeStruct((oh.shape[0], sent), BF16),
        ),
        grid=(requests // batch,),
        in_specs=[whole(a.shape) for a in small]
        + [pl.BlockSpec((batch,) + states.shape[1:], lambda i: (i, 0, 0, 0))],
        out_specs=(
            pl.BlockSpec((rows, heads * size), lambda i: (0, 0)),
            pl.BlockSpec((oh.shape[0], sent), lambda i: (0, 0)),
        ),
        scratch_shapes=[
            pltpu.VMEM((key_heads, requests * slots, size), F32),
            pltpu.VMEM((heads, requests * slots, size), F32),
            pltpu.VMEM((rows, heads * size), F32),
            pltpu.VMEM((rows, heads * size), F32),
            pltpu.VMEM((rows, 2 * heads), F32),
            pltpu.VMEM((rows, 2 * heads), F32),
            pltpu.VMEM((requests, width), BF16),
        ],
        compiler_params=pltpu.CompilerParams(vmem_limit_bytes=40 * 1024 * 1024),
        name="verify_window",
    )(*small, states)


def place_kernel(dims, count, kind_ref, *refs):
    requests, window, heads, key_heads, size, span, needed, lines, batch = dims
    refs = refs[count:]
    oh_ref, pay_ref = refs[:2]
    sources = refs[2 : 2 + count * batch]
    out_ref, kt_ref, vt_ref, k_s, d_s, w_s = refs[2 + count * batch :]
    ratio = heads // key_heads
    o_key, o_delta, o_scale, o_kt, o_vt, width = layout(
        key_heads, heads, window, span, size, needed
    )
    step = pl.program_id(0)

    @pl.when(step == 0)
    def _():
        k_s[...] = jnp.zeros_like(k_s)
        d_s[...] = jnp.zeros_like(d_s)

        def columns(lo, hi):
            return jnp.dot(oh_ref[...], pay_ref[:, lo:hi], preferred_element_type=F32)

        for kh in range(key_heads):
            for j in range(window):
                at = o_key + (kh * window + j) * size
                k_s[kh, pl.ds(j, requests, stride=lines), :] = columns(at, at + size)
        for h in range(heads):
            for j in range(window):
                at = o_delta + (h * window + j) * size
                d_s[h, pl.ds(j, requests, stride=lines), :] = columns(at, at + size)
            at = o_scale + h * size
            w_s[h] = columns(at, at + size)
        kt_ref[...] = columns(o_kt, o_vt).astype(BF16)
        vt_ref[...] = columns(o_vt, width).astype(BF16)

    def apply(slot, source_ref):
        index = step * batch + slot
        row = pl.multiple_of(index * lines, lines)
        for h in range(heads):
            k = k_s[h // ratio, pl.ds(row, lines), :].astype(BF16)
            d = d_s[h, pl.ds(row, lines), :].astype(BF16)
            update = lax.dot_general(
                k, d, (((0,), (0,)), ((), ())), preferred_element_type=F32
            )
            weight = w_s[h, pl.ds(index, 1), :]
            out_ref[slot, h] = weight * source_ref[0, h].astype(F32) + update

    for slot in range(batch):
        kind = kind_ref[step * batch + slot]
        for value in range(count):

            @pl.when(kind == value)
            def _(slot=slot, source_ref=sources[value * batch + slot]):
                apply(slot, source_ref)


def place(dims, kind, indexes, oh, pay, sources):
    requests, _, heads, key_heads, size, span, needed, lines, batch = dims
    block = sources[0].shape[1:]
    count = len(sources)

    def whole(shape):
        return pl.BlockSpec(
            shape, lambda i, *_, n=len(shape): (0,) * n, pipeline_mode=pl.Buffered(1)
        )

    return pl.pallas_call(
        functools.partial(place_kernel, dims, count),
        out_shape=(
            jax.ShapeDtypeStruct((requests,) + block, F32),
            jax.ShapeDtypeStruct((requests, span * needed), BF16),
            jax.ShapeDtypeStruct((requests, span * heads * size), BF16),
        ),
        grid_spec=pltpu.PrefetchScalarGridSpec(
            num_scalar_prefetch=1 + count,
            grid=(requests // batch,),
            in_specs=[whole(oh.shape), whole(pay.shape)]
            + [
                pl.BlockSpec(
                    (1,) + block,
                    lambda i, kind, *index, v=v, j=j: (index[v][i * batch + j], 0, 0, 0),
                )
                for v in range(count)
                for j in range(batch)
            ],
            out_specs=(
                pl.BlockSpec((batch,) + block, lambda i, *_: (i, 0, 0, 0)),
                pl.BlockSpec((requests, span * needed), lambda i, *_: (0, 0)),
                pl.BlockSpec((requests, span * heads * size), lambda i, *_: (0, 0)),
            ),
            scratch_shapes=[
                pltpu.VMEM((key_heads, requests * lines, size), F32),
                pltpu.VMEM((heads, requests * lines, size), F32),
                pltpu.VMEM((heads, requests, size), F32),
            ],
        ),
        compiler_params=pltpu.CompilerParams(vmem_limit_bytes=40 * 1024 * 1024),
        name="place_states",
    )(kind, *indexes, oh, pay, *[source for source in sources for _ in range(batch)])


def local(
    hidden,
    w_key,
    w_value,
    w_gates,
    conv_key,
    conv_value,
    key_conv_state,
    value_conv_state,
    states,
    a_log,
    dt_bias,
    norm_weight,
    w_out,
    accepted,
    next_group,
    next_slot,
):
    requests, window, feature_piece = hidden.shape
    rows = requests * window
    heads = states.shape[1]
    size = states.shape[2]
    span = key_conv_state.shape[1]
    devices = lax.axis_size("head")
    position = lax.axis_index("head")
    groups = lax.axis_size("req")
    group = lax.axis_index("req")
    pair_width = 2 * size
    key_heads = max(1, heads // 2)
    needed = key_heads * pair_width
    own_width = key_conv_state.shape[2] // devices
    column_start = (position * heads // 2) * pair_width
    share = min(CAP, requests // groups)
    extra = CAP - share

    onehot = (next_group[:, None] == jnp.arange(groups, dtype=jnp.int32)[None, :]).astype(jnp.int32)
    before = jnp.cumsum(onehot, axis=0) - onehot
    rank = jnp.sum(before * onehot, axis=1)
    matched = (next_group[None, None, :] == jnp.arange(groups, dtype=jnp.int32)[:, None, None]) & (
        rank[None, None, :] == jnp.arange(CAP, dtype=jnp.int32)[None, :, None]
    )
    picked = jnp.sum(
        matched.astype(jnp.int32) * jnp.arange(requests, dtype=jnp.int32)[None, None, :], axis=2
    )

    moves = {}
    for shift in range(1, groups):
        moves[shift] = [(s, (s + shift) % groups) for s in range(groups)]
    order = sorted(moves, key=lambda shift: (abs(2 * shift - groups), shift))
    sends = {}
    for shift in order:
        rows_out = lax.dynamic_index_in_dim(
            picked[:, :share], (group + shift) % groups, 0, keepdims=False
        )
        sends[shift] = pack(states, rows_out)
    sends, hidden, w_key, w_value, w_gates, key_conv_state, value_conv_state = (
        lax.optimization_barrier(
            (sends, hidden, w_key, w_value, w_gates, key_conv_state, value_conv_state)
        )
    )
    base = {}
    for shift in order:
        base[shift] = lax.ppermute(sends[shift], "req", moves[shift])

    own_rows = jnp.swapaxes(hidden, 0, 1).reshape(rows, feature_piece)
    gathered = lax.all_gather(own_rows, "head", axis=0)
    spread = spread_heads(w_key, devices, key_heads, pair_width)
    columns = lax.all_to_all(spread, "head", split_axis=1, concat_axis=0, tiled=True)
    own_plan = jnp.concatenate([next_group, next_slot]).astype(F32)
    own_plan = jnp.pad(own_plan, (0, -own_plan.shape[0] % 128))[None, :]

    local_state = lax.dynamic_slice_in_dim(key_conv_state, column_start, needed, 2)
    local_taps = lax.dynamic_slice_in_dim(conv_key, column_start, needed, 1)
    send_rows = matched.reshape(groups * CAP, requests).astype(BF16)
    dims = (requests, window, heads, key_heads, size, span, needed, min(8, requests), 16)
    normed, pay = verify(
        dims,
        gathered,
        columns,
        w_value.reshape(devices * feature_piece, heads * 2 * size),
        w_gates.reshape(devices * feature_piece, heads * 2),
        local_taps,
        conv_value,
        jnp.swapaxes(local_state, 0, 1),
        jnp.swapaxes(value_conv_state, 0, 1),
        jnp.repeat(a_log, 2)[None, :],
        jnp.repeat(dt_bias, 2)[None, :],
        norm_weight[None, :],
        accepted[:, None],
        send_rows,
        own_plan,
        states,
    )
    partial_out = jnp.dot(normed, w_out, preferred_element_type=F32)
    mixed = lax.psum_scatter(partial_out, "head", scatter_dimension=1, tiled=True).astype(BF16)
    mixed = jnp.swapaxes(mixed.reshape(window, requests, -1), 0, 1)
    pay_in = lax.all_to_all(pay, "req", split_axis=0, concat_axis=0, tiled=True)
    plan_at = pay.shape[1] - own_plan.shape[1]
    plan = pay_in[::CAP, plan_at : plan_at + 2 * requests].astype(jnp.int32)
    plan = plan.reshape(groups, 2, requests)

    groups_of, slots_of = plan[:, 0], plan[:, 1]
    mine = (groups_of == group).astype(jnp.int32)
    ranks = jnp.cumsum(mine, axis=1) - mine
    hit = (mine[None] > 0) & (slots_of[None] == jnp.arange(requests, dtype=jnp.int32)[:, None, None])
    hit = hit.astype(jnp.int32)
    source = jnp.sum(hit * jnp.arange(groups, dtype=jnp.int32)[None, :, None], axis=(1, 2))
    place_rank = jnp.sum(hit * ranks[None], axis=(1, 2))
    origin = jnp.sum(hit * jnp.arange(requests, dtype=jnp.int32)[None, None, :], axis=(1, 2))
    row_of = source * CAP + place_rank
    take_rows = (row_of[:, None] == jnp.arange(groups * CAP, dtype=jnp.int32)[None, :]).astype(BF16)
    shift_in = (group - source + groups) % groups
    kind = jnp.where(shift_in == 0, 0, jnp.where(place_rank < share, shift_in, groups - 1 + shift_in))
    kind = kind.astype(jnp.int32)

    counts = jnp.sum(
        (groups_of[:, None, :] == jnp.arange(groups, dtype=jnp.int32)[None, :, None]).astype(
            jnp.int32
        ),
        axis=2,
    )
    shifts = (
        jnp.arange(groups, dtype=jnp.int32)[None, :]
        - jnp.arange(groups, dtype=jnp.int32)[:, None]
        + groups
    ) % groups
    extra_block = (max(extra, 1),) + states.shape[1:]
    late = []
    pick_extra = picked[:, share:]
    pick_extra, counts, _ = lax.optimization_barrier((pick_extra, counts, partial_out))
    for shift in range(1, groups):
        most = jnp.max(jnp.where(shifts == shift, counts, 0))

        def send(pick, source_states, pairs=moves[shift], shift=shift):
            rows_out = lax.dynamic_index_in_dim(pick, (group + shift) % groups, 0, keepdims=False)
            return lax.ppermute(pack(source_states, rows_out), "req", pairs)

        def skip(pick, source_states):
            return jnp.zeros(extra_block, BF16)

        if extra > 0:
            late.append(lax.cond(most > share, send, skip, pick_extra, states))
        else:
            late.append(jnp.zeros(extra_block, BF16))

    batch = 4 if requests % 4 == 0 else 1
    wanted = jnp.where(
        kind == 0,
        origin,
        jnp.where(kind < groups, place_rank, place_rank - share),
    ).astype(jnp.int32)
    limit = max(requests, groups * CAP)
    turn = jnp.arange(requests, dtype=jnp.int32) // batch
    used = kind[None, :] == jnp.arange(2 * groups - 1, dtype=jnp.int32)[:, None]
    coded = jnp.where(used, (turn * limit + wanted)[None, :], 0)
    coded = lax.cummax(coded.reshape(2 * groups - 1, requests // batch, batch), axis=1)
    indexes = lax.rem(coded, limit).reshape(2 * groups - 1, requests)
    dims = (requests, window, heads, key_heads, size, span, needed, 8, batch)
    new_states, key_rows, value_rows = place(
        dims,
        kind,
        [indexes[v] for v in range(2 * groups - 1)],
        take_rows,
        pay_in,
        [states] + [base[shift] for shift in range(1, groups)] + late,
    )
    new_key = key_rows.reshape(requests, span, needed)
    if own_width != needed:
        new_key = lax.dynamic_slice_in_dim(
            new_key, position * own_width - column_start, own_width, 2
        )
    new_value = value_rows.reshape(requests, span, heads * size)
    return (mixed, new_states, new_key, new_value)


def solution(mesh):
    in_specs = (
        P("req", None, "head"),
        P("head", None),
        P(None, "head", None),
        P(None, "head", None),
        P(),
        P(None, "head"),
        P("req", None, None),
        P("req", None, "head"),
        P("req", "head", None, None),
        P("head"),
        P("head"),
        P(),
        P("head", None),
        P("req"),
        P("req"),
        P("req"),
    )
    out_specs = (
        P("req", None, "head"),
        P("req", "head", None, None),
        P("req", None, "head"),
        P("req", None, "head"),
    )

    return jax.shard_map(local, mesh=mesh, in_specs=in_specs, out_specs=out_specs, check_vma=False)
```

```python
import functools

import jax
import jax.numpy as jnp
from jax import lax
from jax.experimental import pallas as pl
from jax.experimental.pallas import tpu as pltpu
from jax.sharding import PartitionSpec as P


CAP = 12
F32 = jnp.float32
BF16 = jnp.bfloat16


def spread_heads(block, devices, key_heads, pair_width):
    rows = block.shape[0]
    shaped = block.reshape(rows, -1, pair_width)
    wanted = devices * key_heads
    if shaped.shape[1] < wanted:
        shaped = jnp.repeat(shaped, wanted // shaped.shape[1], axis=1)
    return shaped.reshape(rows, wanted * pair_width)


def silu(x):
    return x / (1.0 + jnp.exp(-x))


def pack_kernel(index_ref, *refs):
    out_ref = refs[-1]
    for row, in_ref in enumerate(refs[:-1]):
        out_ref[row] = in_ref[0].astype(out_ref.dtype)


def pack(states, picked):
    count = picked.shape[0]
    batch = 4 if count % 4 == 0 else 1
    block = states.shape[1:]
    zeros = (0,) * len(block)
    return pl.pallas_call(
        pack_kernel,
        out_shape=jax.ShapeDtypeStruct((count,) + block, BF16),
        grid_spec=pltpu.PrefetchScalarGridSpec(
            num_scalar_prefetch=1,
            grid=(count // batch,),
            in_specs=[
                pl.BlockSpec((1,) + block, lambda i, index, j=j: (index[i * batch + j],) + zeros)
                for j in range(batch)
            ],
            out_specs=pl.BlockSpec((batch,) + block, lambda i, index: (i,) + zeros),
        ),
        name="pack_states",
    )(picked, *([states] * batch))


def layout(key_heads, heads, window, span, size, needed):
    keys = 0
    deltas = keys + key_heads * window * size
    scale = deltas + heads * window * size
    key_tail = scale + heads * size
    value_tail = key_tail + span * needed
    return keys, deltas, scale, key_tail, value_tail, value_tail + span * heads * size


def verify_kernel(
    dims,
    x_ref,
    wk_ref,
    wv_ref,
    wg_ref,
    ck_ref,
    cv_ref,
    ks_ref,
    vs_ref,
    al_ref,
    db_ref,
    nw_ref,
    acc_ref,
    oh_ref,
    st_ref,
    normed_ref,
    pay_ref,
    kq_s,
    g_s,
    v_s,
    z_s,
    beta_s,
    decay_s,
    p_s,
):
    requests, window, heads, key_heads, size, span, needed, batch, slots = dims
    half = slots // 2
    ratio = heads // key_heads
    devices, _, piece = x_ref.shape
    o_key, o_delta, o_scale, o_kt, o_vt, _ = layout(key_heads, heads, window, span, size, needed)
    step = pl.program_id(0)

    def project(w_ref, lo, width):
        total = jnp.dot(
            x_ref[0], w_ref[0:piece, lo : lo + width], preferred_element_type=F32
        )
        for d in range(1, devices):
            total = total + jnp.dot(
                x_ref[d],
                w_ref[d * piece : (d + 1) * piece, lo : lo + width],
                preferred_element_type=F32,
            )
        return total.astype(BF16).astype(F32)

    def conv(state_ref, taps_ref, raw, lo, width, tail_at, tail_width):
        u = [state_ref[i, :, lo : lo + width].astype(F32) for i in range(span)]
        u += [raw[t * requests : (t + 1) * requests] for t in range(window)]
        outs = []
        for t in range(window):
            total = taps_ref[0:1, lo : lo + width].astype(F32) * u[t]
            for i in range(1, span + 1):
                total = total + taps_ref[i : i + 1, lo : lo + width].astype(F32) * u[t + i]
            outs.append(silu(total).astype(BF16).astype(F32))
        accepted = acc_ref[...]
        for i in range(span):
            tail = u[1 + i]
            for a in range(1, window):
                tail = jnp.where(accepted == a, u[a + 1 + i], tail)
            at = tail_at + i * tail_width + lo
            p_s[:, at : at + width] = tail.astype(BF16)
        return outs

    @pl.when(step == 0)
    def _():
        kq_s[...] = jnp.zeros_like(kq_s)
        for kh in range(key_heads):
            width = 2 * size
            raw = project(wk_ref, kh * width, width)
            outs = conv(ks_ref, ck_ref, raw, kh * width, width, o_kt, needed)
            for t in range(window):
                q = outs[t][:, :size]
                k = outs[t][:, size:]
                q = q * lax.rsqrt(jnp.sum(q * q, axis=-1, keepdims=True) + 1e-06)
                k = k * lax.rsqrt(jnp.sum(k * k, axis=-1, keepdims=True) + 1e-06)
                kq_s[kh, pl.ds(t, requests, stride=slots), :] = k
                kq_s[kh, pl.ds(half + t, requests, stride=slots), :] = q * size ** (-0.5)
        for h in range(heads):
            raw = project(wv_ref, h * 2 * size, 2 * size)
            zg = raw[:, size:]
            z_s[:, h * size : (h + 1) * size] = silu(zg)
            outs = conv(vs_ref, cv_ref, raw[:, :size], h * size, size, o_vt, heads * size)
            for t in range(window):
                v_s[t * requests : (t + 1) * requests, h * size : (h + 1) * size] = outs[t]
        gates = project(wg_ref, 0, 2 * heads)
        beta_s[...] = 1.0 / (1.0 + jnp.exp(-gates))
        shifted = gates + db_ref[...]
        soft = jnp.maximum(shifted, 0.0) + jnp.log1p(jnp.exp(-jnp.abs(shifted)))
        decay_s[...] = jnp.exp(-jnp.exp(al_ref[...]) * soft)

    for rr in range(batch):
        row = pl.multiple_of((step * batch + rr) * slots, slots)
        for kh in range(key_heads):
            lhs = kq_s[kh, pl.ds(row, slots), :].astype(BF16)
            rhs = jnp.concatenate(
                [st_ref[rr, kh * ratio + e].astype(BF16) for e in range(ratio)], axis=1
            )
            got = jnp.dot(lhs, rhs, preferred_element_type=F32)
            for e in range(ratio):
                g_s[kh * ratio + e, pl.ds(row, slots), :] = got[:, e * size : (e + 1) * size]

    @pl.when(step == pl.num_programs(0) - 1)
    def _():
        accepted = acc_ref[...]
        gain = nw_ref[...]
        for kh in range(key_heads):
            ks = [kq_s[kh, pl.ds(t, requests, stride=slots), :] for t in range(window)]
            qs = [kq_s[kh, pl.ds(half + t, requests, stride=slots), :] for t in range(window)]
            kk = {}
            kq = {}
            for t in range(window):
                at = o_key + (kh * window + t) * size
                p_s[:, at : at + size] = ks[t].astype(BF16)
                for j in range(t + 1):
                    if j < t:
                        kk[t, j] = jnp.sum(ks[t] * ks[j], axis=-1, keepdims=True)
                    kq[t, j] = jnp.sum(qs[t] * ks[j], axis=-1, keepdims=True)
            for e in range(ratio):
                h = kh * ratio + e
                cols = slice(h * size, (h + 1) * size)
                deltas = []
                coef = []
                whole = None
                kept_coef = [None] * window
                kept_whole = None
                for t in range(window):
                    rows = slice(t * requests, (t + 1) * requests)
                    beta = beta_s[rows, 2 * h : 2 * h + 1]
                    decay = decay_s[rows, 2 * h + 1 : 2 * h + 2]
                    whole = decay if t == 0 else whole * decay
                    coef = [c * decay for c in coef]
                    guess = whole * g_s[h, pl.ds(t, requests, stride=slots), :]
                    core = whole * g_s[h, pl.ds(half + t, requests, stride=slots), :]
                    for j in range(t):
                        guess = guess + (coef[j] * kk[t, j]) * deltas[j]
                        core = core + (coef[j] * kq[t, j]) * deltas[j]
                    delta = beta * (v_s[rows, cols] - guess)
                    core = core + kq[t, t] * delta
                    deltas.append(delta)
                    coef.append(jnp.ones_like(decay))
                    here = accepted == t
                    kept_whole = whole if t == 0 else jnp.where(here, whole, kept_whole)
                    for j in range(t + 1):
                        before = kept_coef[j] if kept_coef[j] is not None else jnp.zeros_like(decay)
                        kept_coef[j] = jnp.where(here, coef[j], before)
                    scaled = core * lax.rsqrt(
                        jnp.mean(core * core, axis=-1, keepdims=True) + 1e-06
                    )
                    normed_ref[rows, cols] = (scaled * gain * z_s[rows, cols]).astype(BF16)
                for j in range(window):
                    at = o_delta + (h * window + j) * size
                    p_s[:, at : at + size] = (kept_coef[j] * deltas[j]).astype(BF16)
                at = o_scale + h * size
                p_s[:, at : at + size] = jnp.broadcast_to(kept_whole, (requests, size)).astype(BF16)
        pay_ref[...] = jnp.dot(oh_ref[...], p_s[...], preferred_element_type=F32).astype(BF16)


def verify(dims, x, wk, wv, wg, ck, cv, ks, vs, al, db, nw, acc, oh, states):
    requests, window, heads, key_heads, size, span, needed, batch, slots = dims
    rows = requests * window
    width = layout(key_heads, heads, window, span, size, needed)[-1]
    small = [x, wk, wv, wg, ck, cv, ks, vs, al, db, nw, acc, oh]

    def whole(shape):
        return pl.BlockSpec(
            shape, lambda i, n=len(shape): (0,) * n, pipeline_mode=pl.Buffered(1)
        )

    return pl.pallas_call(
        functools.partial(verify_kernel, dims),
        out_shape=(
            jax.ShapeDtypeStruct((rows, heads * size), BF16),
            jax.ShapeDtypeStruct((oh.shape[0], width), BF16),
        ),
        grid=(requests // batch,),
        in_specs=[whole(a.shape) for a in small]
        + [pl.BlockSpec((batch,) + states.shape[1:], lambda i: (i, 0, 0, 0))],
        out_specs=(
            pl.BlockSpec((rows, heads * size), lambda i: (0, 0)),
            pl.BlockSpec((oh.shape[0], width), lambda i: (0, 0)),
        ),
        scratch_shapes=[
            pltpu.VMEM((key_heads, requests * slots, size), F32),
            pltpu.VMEM((heads, requests * slots, size), F32),
            pltpu.VMEM((rows, heads * size), F32),
            pltpu.VMEM((rows, heads * size), F32),
            pltpu.VMEM((rows, 2 * heads), F32),
            pltpu.VMEM((rows, 2 * heads), F32),
            pltpu.VMEM((requests, width), BF16),
        ],
        compiler_params=pltpu.CompilerParams(vmem_limit_bytes=40 * 1024 * 1024),
        name="verify_window",
    )(*small, states)


def place_kernel(dims, count, kind_ref, *refs):
    requests, window, heads, key_heads, size, span, needed, lines, batch = dims
    refs = refs[count:]
    oh_ref, pay_ref = refs[:2]
    sources = refs[2 : 2 + count * batch]
    out_ref, kt_ref, vt_ref, k_s, d_s, w_s = refs[2 + count * batch :]
    ratio = heads // key_heads
    o_key, o_delta, o_scale, o_kt, o_vt, width = layout(
        key_heads, heads, window, span, size, needed
    )
    step = pl.program_id(0)

    @pl.when(step == 0)
    def _():
        k_s[...] = jnp.zeros_like(k_s)
        d_s[...] = jnp.zeros_like(d_s)

        def columns(lo, hi):
            return jnp.dot(oh_ref[...], pay_ref[:, lo:hi], preferred_element_type=F32)

        for kh in range(key_heads):
            for j in range(window):
                at = o_key + (kh * window + j) * size
                k_s[kh, pl.ds(j, requests, stride=lines), :] = columns(at, at + size)
        for h in range(heads):
            for j in range(window):
                at = o_delta + (h * window + j) * size
                d_s[h, pl.ds(j, requests, stride=lines), :] = columns(at, at + size)
            at = o_scale + h * size
            w_s[h] = columns(at, at + size)
        kt_ref[...] = columns(o_kt, o_vt).astype(BF16)
        vt_ref[...] = columns(o_vt, width).astype(BF16)

    def apply(slot, source_ref):
        index = step * batch + slot
        row = pl.multiple_of(index * lines, lines)
        for kh in range(key_heads):
            k = k_s[kh, pl.ds(row, lines), :].astype(BF16)
            d = jnp.concatenate(
                [d_s[kh * ratio + e, pl.ds(row, lines), :] for e in range(ratio)], axis=1
            ).astype(BF16)
            update = lax.dot_general(
                k, d, (((0,), (0,)), ((), ())), preferred_element_type=F32
            )
            for e in range(ratio):
                h = kh * ratio + e
                weight = w_s[h, pl.ds(index, 1), :]
                part = update[:, e * size : (e + 1) * size]
                out_ref[slot, h] = weight * source_ref[0, h].astype(F32) + part

    for slot in range(batch):
        kind = kind_ref[step * batch + slot]
        for value in range(count):

            @pl.when(kind == value)
            def _(slot=slot, source_ref=sources[value * batch + slot]):
                apply(slot, source_ref)


def place(dims, kind, indexes, oh, pay, sources):
    requests, _, heads, key_heads, size, span, needed, lines, batch = dims
    block = sources[0].shape[1:]
    count = len(sources)

    def whole(shape):
        return pl.BlockSpec(
            shape, lambda i, *_, n=len(shape): (0,) * n, pipeline_mode=pl.Buffered(1)
        )

    return pl.pallas_call(
        functools.partial(place_kernel, dims, count),
        out_shape=(
            jax.ShapeDtypeStruct((requests,) + block, F32),
            jax.ShapeDtypeStruct((requests, span * needed), BF16),
            jax.ShapeDtypeStruct((requests, span * heads * size), BF16),
        ),
        grid_spec=pltpu.PrefetchScalarGridSpec(
            num_scalar_prefetch=1 + count,
            grid=(requests // batch,),
            in_specs=[whole(oh.shape), whole(pay.shape)]
            + [
                pl.BlockSpec(
                    (1,) + block,
                    lambda i, kind, *index, v=v, j=j: (index[v][i * batch + j], 0, 0, 0),
                )
                for v in range(count)
                for j in range(batch)
            ],
            out_specs=(
                pl.BlockSpec((batch,) + block, lambda i, *_: (i, 0, 0, 0)),
                pl.BlockSpec((requests, span * needed), lambda i, *_: (0, 0)),
                pl.BlockSpec((requests, span * heads * size), lambda i, *_: (0, 0)),
            ),
            scratch_shapes=[
                pltpu.VMEM((key_heads, requests * lines, size), F32),
                pltpu.VMEM((heads, requests * lines, size), F32),
                pltpu.VMEM((heads, requests, size), F32),
            ],
        ),
        compiler_params=pltpu.CompilerParams(vmem_limit_bytes=40 * 1024 * 1024),
        name="place_states",
    )(kind, *indexes, oh, pay, *[source for source in sources for _ in range(batch)])


def local(
    hidden,
    w_key,
    w_value,
    w_gates,
    conv_key,
    conv_value,
    key_conv_state,
    value_conv_state,
    states,
    a_log,
    dt_bias,
    norm_weight,
    w_out,
    accepted,
    next_group,
    next_slot,
):
    requests, window, feature_piece = hidden.shape
    rows = requests * window
    heads = states.shape[1]
    size = states.shape[2]
    span = key_conv_state.shape[1]
    devices = lax.axis_size("head")
    position = lax.axis_index("head")
    groups = lax.axis_size("req")
    group = lax.axis_index("req")
    pair_width = 2 * size
    key_heads = max(1, heads // 2)
    needed = key_heads * pair_width
    own_width = key_conv_state.shape[2] // devices
    column_start = (position * heads // 2) * pair_width
    share = min(CAP, requests // groups)
    extra = CAP - share

    onehot = (next_group[:, None] == jnp.arange(groups, dtype=jnp.int32)[None, :]).astype(jnp.int32)
    before = jnp.cumsum(onehot, axis=0) - onehot
    rank = jnp.sum(before * onehot, axis=1)
    matched = (next_group[None, None, :] == jnp.arange(groups, dtype=jnp.int32)[:, None, None]) & (
        rank[None, None, :] == jnp.arange(CAP, dtype=jnp.int32)[None, :, None]
    )
    picked = jnp.sum(
        matched.astype(jnp.int32) * jnp.arange(requests, dtype=jnp.int32)[None, None, :], axis=2
    )

    moves = {}
    for shift in range(1, groups):
        moves[shift] = [(s, (s + shift) % groups) for s in range(groups)]
    order = sorted(moves, key=lambda shift: (abs(2 * shift - groups), shift))
    sends = {}
    for shift in order:
        rows_out = lax.dynamic_index_in_dim(
            picked[:, :share], (group + shift) % groups, 0, keepdims=False
        )
        sends[shift] = pack(states, rows_out)
    last = order[-1]
    own_plan = jnp.stack([next_group, next_slot])
    sends[last], own_plan, hidden, w_key, w_value, w_gates, key_conv_state, value_conv_state = (
        lax.optimization_barrier(
            (
                sends[last],
                own_plan,
                hidden,
                w_key,
                w_value,
                w_gates,
                key_conv_state,
                value_conv_state,
            )
        )
    )
    base = {}
    plans = [own_plan]
    for shift in order:
        base[shift] = lax.ppermute(sends[shift], "req", moves[shift])
    for shift in range(1, groups):
        plans.append(lax.ppermute(own_plan, "req", moves[shift]))

    own_rows = jnp.swapaxes(hidden, 0, 1).reshape(rows, feature_piece)
    gathered = lax.all_gather(own_rows, "head", axis=0)
    spread = spread_heads(w_key, devices, key_heads, pair_width)
    columns = lax.all_to_all(spread, "head", split_axis=1, concat_axis=0, tiled=True)
    local_state = lax.dynamic_slice_in_dim(key_conv_state, column_start, needed, 2)
    local_taps = lax.dynamic_slice_in_dim(conv_key, column_start, needed, 1)
    send_rows = matched.reshape(groups * CAP, requests).astype(BF16)
    dims = (requests, window, heads, key_heads, size, span, needed, min(8, requests), 16)
    normed, pay = verify(
        dims,
        gathered,
        columns,
        w_value.reshape(devices * feature_piece, heads * 2 * size),
        w_gates.reshape(devices * feature_piece, heads * 2),
        local_taps,
        conv_value,
        jnp.swapaxes(local_state, 0, 1),
        jnp.swapaxes(value_conv_state, 0, 1),
        jnp.repeat(a_log, 2)[None, :],
        jnp.repeat(dt_bias, 2)[None, :],
        norm_weight[None, :],
        accepted[:, None],
        send_rows,
        states,
    )
    partial_out = jnp.dot(normed, w_out, preferred_element_type=F32)
    mixed = lax.psum_scatter(partial_out, "head", scatter_dimension=1, tiled=True).astype(BF16)
    mixed = jnp.swapaxes(mixed.reshape(window, requests, -1), 0, 1)
    pay_in = lax.all_to_all(pay, "req", split_axis=0, concat_axis=0, tiled=True)

    plan = jnp.stack(plans)
    came = (group - jnp.arange(groups, dtype=jnp.int32) + groups) % groups
    arrived = came[:, None] == jnp.arange(groups, dtype=jnp.int32)[None, :]
    plan = jnp.sum(jnp.where(arrived[:, :, None, None], plan[None], 0), axis=1)
    groups_of, slots_of = plan[:, 0], plan[:, 1]
    mine = (groups_of == group).astype(jnp.int32)
    ranks = jnp.cumsum(mine, axis=1) - mine
    hit = (mine[None] > 0) & (slots_of[None] == jnp.arange(requests, dtype=jnp.int32)[:, None, None])
    hit = hit.astype(jnp.int32)
    source = jnp.sum(hit * jnp.arange(groups, dtype=jnp.int32)[None, :, None], axis=(1, 2))
    place_rank = jnp.sum(hit * ranks[None], axis=(1, 2))
    origin = jnp.sum(hit * jnp.arange(requests, dtype=jnp.int32)[None, None, :], axis=(1, 2))
    row_of = source * CAP + place_rank
    take_rows = (row_of[:, None] == jnp.arange(groups * CAP, dtype=jnp.int32)[None, :]).astype(BF16)
    shift_in = (group - source + groups) % groups
    kind = jnp.where(shift_in == 0, 0, jnp.where(place_rank < share, shift_in, groups - 1 + shift_in))
    kind = kind.astype(jnp.int32)

    counts = jnp.sum(
        (groups_of[:, None, :] == jnp.arange(groups, dtype=jnp.int32)[None, :, None]).astype(
            jnp.int32
        ),
        axis=2,
    )
    shifts = (
        jnp.arange(groups, dtype=jnp.int32)[None, :]
        - jnp.arange(groups, dtype=jnp.int32)[:, None]
        + groups
    ) % groups
    extra_block = (max(extra, 1),) + states.shape[1:]
    late = []
    pick_extra = picked[:, share:]
    pick_extra, counts, _ = lax.optimization_barrier((pick_extra, counts, partial_out))
    for shift in range(1, groups):
        most = jnp.max(jnp.where(shifts == shift, counts, 0))

        def send(pick, source_states, pairs=moves[shift], shift=shift):
            rows_out = lax.dynamic_index_in_dim(pick, (group + shift) % groups, 0, keepdims=False)
            return lax.ppermute(pack(source_states, rows_out), "req", pairs)

        def skip(pick, source_states):
            return jnp.zeros(extra_block, BF16)

        if extra > 0:
            late.append(lax.cond(most > share, send, skip, pick_extra, states))
        else:
            late.append(jnp.zeros(extra_block, BF16))

    batch = 4 if requests % 4 == 0 else 1
    wanted = jnp.where(
        kind == 0,
        origin,
        jnp.where(kind < groups, place_rank, place_rank - share),
    ).astype(jnp.int32)
    limit = max(requests, groups * CAP)
    turn = jnp.arange(requests, dtype=jnp.int32) // batch
    used = kind[None, :] == jnp.arange(2 * groups - 1, dtype=jnp.int32)[:, None]
    coded = jnp.where(used, (turn * limit + wanted)[None, :], 0)
    coded = lax.cummax(coded.reshape(2 * groups - 1, requests // batch, batch), axis=1)
    indexes = lax.rem(coded, limit).reshape(2 * groups - 1, requests)
    dims = (requests, window, heads, key_heads, size, span, needed, 8, batch)
    kind, mixed = lax.optimization_barrier((kind, mixed))
    new_states, key_rows, value_rows = place(
        dims,
        kind,
        [indexes[v] for v in range(2 * groups - 1)],
        take_rows,
        pay_in,
        [states] + [base[shift] for shift in range(1, groups)] + late,
    )
    new_key = key_rows.reshape(requests, span, needed)
    if own_width != needed:
        new_key = lax.dynamic_slice_in_dim(
            new_key, position * own_width - column_start, own_width, 2
        )
    new_value = value_rows.reshape(requests, span, heads * size)
    return (mixed, new_states, new_key, new_value)


def solution(mesh):
    in_specs = (
        P("req", None, "head"),
        P("head", None),
        P(None, "head", None),
        P(None, "head", None),
        P(),
        P(None, "head"),
        P("req", None, None),
        P("req", None, "head"),
        P("req", "head", None, None),
        P("head"),
        P("head"),
        P(),
        P("head", None),
        P("req"),
        P("req"),
        P("req"),
    )
    out_specs = (
        P("req", None, "head"),
        P("req", "head", None, None),
        P("req", None, "head"),
        P("req", None, "head"),
    )

    return jax.shard_map(local, mesh=mesh, in_specs=in_specs, out_specs=out_specs, check_vma=False)
```
